32 devices in a mesh: slab: 8 (over y, x, core), lat: 4 (over z).
Axes of the slice: x: 2, y: 2, z: 4, core: 2. Of those that a mesh axis runs over, the one named last changes fastest.
Arguments:
- tokens: bfloat16 [16, 16, 16, 1024], P(None, 'lat', 'slab'), may hold values from -6 to 6
- conv_first: float32 [27, 1024], replicated, may hold values from -1.25 to 1.25
- conv_second: float32 [27, 1024], replicated, may hold values from -1.25 to 1.25
- kv_weight: bfloat16 [2, 1024, 1024], P(None, None, 'lat'), may hold values from -0.1875 to 0.1875
- queries: bfloat16 [512, 1024], replicated, may hold values from -70 to 70
Outputs:
- decoded: bfloat16 [16, 16, 16, 1024], P(None, 'lat', 'slab')
The draws below stay inside these ranges and needn't reach their ends.
All inputs are finite; a program needn't handle non-finite values.
Results may differ from the reference program's by a relative error of at most 0.012.
The reference program's roundings to bfloat16 on the way (of `inner`, `hidden`, `weights`, `latents` and `probs`) count: a program that leaves them out, or rounds other values in their place, can miss the bound.
Values may be sent and summed in bfloat16 or wider, within the bound.
No kernel may reach another device: no remote copies, remote signals or barrier semaphores. Data moves between devices by JAX's collectives and lax.ppermute only.
A program may use at most 64 MiB of HBM per device.

```python
import jax
import jax.numpy as jnp
from jax import lax

D = 1024
LATENTS = 512
TAPS = 27
NX = 16
NY = 16
NZ = 16


def draw_queries(key, part):
    first_key = jax.random.fold_in(jax.random.fold_in(key, 17), 0)
    values = 4.0 * jnp.clip(jax.random.normal(first_key, (LATENTS, D), jnp.float32), -6.0, 6.0)
    return values.astype(jnp.bfloat16)


def levels(stream_key, dims, pieces, least, high):
    gain = 1.0
    for position, blocks in pieces:
        draws = jax.random.uniform(jax.random.fold_in(jax.random.fold_in(stream_key, 6), position), (blocks,), jnp.float32, least / len(pieces), high / len(pieces))
        gain = gain * jnp.repeat(jnp.exp(draws), dims[position] // blocks).reshape((-1,) + (1,) * (len(dims) - 1 - position))
    return gain


def normal_values(own_key, dims, scale, most, shards=(), kind=jnp.bfloat16):
    values = jax.random.normal(own_key, dims, jnp.float32) * scale
    if len(shards) > 0:
        values = levels(own_key, dims, shards, -0.22, 0.18) * values
    return jnp.clip(values, min=-most, max=most).astype(kind)


def setup_inputs(seed: int = 0) -> dict:
    seeds = jax.random.split(jax.random.key(seed), 6)
    tokens = normal_values(seeds[0], (NX, NY, NZ, D), 1.0, 6.0, ((1, 4), (2, 8)))
    conv_first = normal_values(seeds[1], (TAPS, D), TAPS ** -0.5, 1.25, (), jnp.float32)
    conv_second = normal_values(seeds[2], (TAPS, D), TAPS ** -0.5, 1.25, (), jnp.float32)
    kv_weight = normal_values(seeds[3], (2, D, D), D ** -0.5, 0.1875, ((2, 4),))
    queries = draw_queries(jax.random.fold_in(seeds[5], 71), 0)
    return dict(tokens=tokens, conv_first=conv_first, conv_second=conv_second, kv_weight=kv_weight, queries=queries)


def conv_same(field, weights):
    padded = jnp.pad(field, ((1, 1), (1, 1), (1, 1), (0, 0)))
    size_x, size_y, size_z = field.shape[0], field.shape[1], field.shape[2]
    accum_sum = jnp.zeros(field.shape, jnp.float32)
    for tap_index in range(27):
        shift_x = tap_index // 9
        shift_y = (tap_index // 3) % 3
        shift_z = tap_index % 3
        window = padded[shift_x:shift_x + size_x, shift_y:shift_y + size_y, shift_z:shift_z + size_z]
        accum_sum = accum_sum + weights[tap_index] * window
    return accum_sum


def reference(tokens, conv_first, conv_second, kv_weight, queries):
    source = tokens.astype(jnp.float32)
    inner = jax.nn.gelu(conv_same(source, conv_first)).astype(jnp.bfloat16)
    mixed = jax.nn.gelu(conv_same(inner.astype(jnp.float32), conv_second))
    hidden = (source + mixed).astype(jnp.bfloat16)
    width = hidden.shape[3]
    token_rows = hidden.reshape(-1, width)
    block_size = min(8192, token_rows.shape[0])
    blocked = token_rows.reshape(-1, block_size, width)
    score_scale = 1.0 / (width ** 0.5)

    def encode(carry, block_rows):
        maximum, denominator, numerator = carry
        key_rows = jnp.dot(block_rows, kv_weight[0], preferred_element_type=jnp.float32).astype(jnp.bfloat16)
        value_rows = jnp.dot(block_rows, kv_weight[1], preferred_element_type=jnp.float32).astype(jnp.bfloat16)
        scores = jnp.dot(queries, key_rows.T, preferred_element_type=jnp.float32) * score_scale
        new_max = jnp.maximum(maximum, jnp.max(scores, axis=1))
        rescale = jnp.exp(maximum - new_max)
        exponent = jnp.exp(scores - new_max[:, None])
        weights_bf = exponent.astype(jnp.bfloat16)
        denominator = denominator * rescale + jnp.sum(exponent, axis=1)
        numerator = numerator * rescale[:, None] + jnp.dot(weights_bf, value_rows, preferred_element_type=jnp.float32)
        return (new_max, denominator, numerator), None

    start_carry = (jnp.full((queries.shape[0],), -jnp.inf, jnp.float32),
                   jnp.zeros((queries.shape[0],), jnp.float32),
                   jnp.zeros((queries.shape[0], width), jnp.float32))
    (maximum, denominator, numerator), unused = lax.scan(encode, start_carry, blocked)
    latents = (numerator / denominator[:, None]).astype(jnp.bfloat16)

    def decode(block_rows):
        back = jnp.dot(block_rows, latents.T, preferred_element_type=jnp.float32) * score_scale
        probs = jax.nn.softmax(back, axis=1).astype(jnp.bfloat16)
        result = block_rows.astype(jnp.float32) + jnp.dot(probs, latents, preferred_element_type=jnp.float32)
        return result.astype(jnp.bfloat16)

    decoded = lax.map(decode, blocked)
    return decoded.reshape(hidden.shape)
```

```python
import functools

import jax
import jax.numpy as jnp
from jax import lax
from jax.experimental import pallas as pl
from jax.experimental.pallas import tpu as pltpu
from jax.sharding import PartitionSpec as P

F32 = jnp.float32
BF16 = jnp.bfloat16
LANES = 128
VMEM = pltpu.VMEM


def dot(a, b, contract):
    return lax.dot_general(a, b, (contract, ((), ())), preferred_element_type=F32)


def radices(count):
    found, stride = [], 1
    while stride < count:
        radix = 4 if count // stride % 4 == 0 else 2
        found.append((stride, radix))
        stride *= radix
    return found


def swap(block, axis, bits):
    count = lax.axis_size(axis)
    return lax.ppermute(block, axis, [(i, i ^ bits) for i in range(count)])


def gather_relative(block, axis, stages):
    for stride, radix in stages:
        received = [swap(block, axis, k * stride) for k in range(1, radix)]
        block = jnp.stack([block] + received)
    return block


def partner(position, count, near):
    other = position ^ 1 if near else ((position + 1) ^ 1) - 1
    return other if 0 <= other < count else None


def pair_exchange(block, axis, near):
    count = lax.axis_size(axis)
    pairs = [(partner(i, count, near), i) for i in range(count)]
    return lax.ppermute(block, axis, [p for p in pairs if p[0] is not None])


def conv_kernel(flags, own, near, far, near_rows, far_rows, first, second, out, cells, inner):
    size_y, size_z, size_x, _ = own.shape
    low_y, high_y, low_z, high_z = flags[0], flags[1], flags[2], flags[3]
    near_z, far_z, near_y, far_y = flags[4], flags[5], flags[6], flags[7]
    cells[2 : 2 + size_y, 2 : 2 + size_z] = own[...].astype(F32)
    cells[2 : 2 + size_y, pl.ds(near_z, 2)] = near[...].astype(F32)
    cells[2 : 2 + size_y, pl.ds(far_z, 2)] = far[...].astype(F32)
    for rows, start in ((near_rows, near_y), (far_rows, far_y)):
        cells[pl.ds(start, 2), 2 : 2 + size_z] = rows[0].astype(F32)
        cells[pl.ds(start, 2), pl.ds(near_z, 2)] = rows[1].astype(F32)
        cells[pl.ds(start, 2), pl.ds(far_z, 2)] = rows[2].astype(F32)

    def conv(source, weights, y, breadth):
        parts = [None, None, None]
        for b in range(3):
            for c in range(3):
                window = source[y + b, c : c + breadth]
                for a in range(3):
                    tap = 9 * a + 3 * b + c
                    term = weights[tap : tap + 1, :][None] * window
                    parts[a] = term if parts[a] is None else parts[a] + term
        place = lax.broadcasted_iota(jnp.int32, parts[0].shape, 1)
        before = jnp.where(place == 0, 0.0, pltpu.roll(parts[0], 1, 1))
        after = jnp.where(place == size_x - 1, 0.0, pltpu.roll(parts[2], size_x - 1, 1))
        return before + parts[1] + after

    for y in range(size_y + 2):
        value = jax.nn.gelu(conv(cells, first, y, size_z + 2)).astype(BF16).astype(F32)
        if y == 0:
            value = jnp.where(low_y > 0, value, 0.0)
        if y == size_y + 1:
            value = jnp.where(high_y > 0, value, 0.0)
        inner[y] = value
        inner[y, 0] = jnp.where(low_z > 0, inner[y, 0], 0.0)
        inner[y, size_z + 1] = jnp.where(high_z > 0, inner[y, size_z + 1], 0.0)
    for y in range(size_y):
        mixed = jax.nn.gelu(conv(inner, second, y, size_z))
        out[y] = (cells[y + 2, 2 : 2 + size_z] + mixed).astype(BF16)


def hidden_of(flags, own, pieces, first, second):
    size_y, size_z, size_x, width = own.shape
    lanes = LANES

    def spec(array):
        ahead = array.shape[:-1]
        return pl.BlockSpec(ahead + (lanes,), lambda i: (0,) * len(ahead) + (i,))

    weight_spec = pl.BlockSpec((first.shape[0], lanes), lambda i: (0, i))
    arrays = [own] + pieces
    return pl.pallas_call(
        conv_kernel,
        grid=(width // lanes,),
        out_shape=jax.ShapeDtypeStruct(own.shape, BF16),
        in_specs=[pl.BlockSpec(memory_space=pltpu.SMEM)]
        + [spec(a) for a in arrays]
        + [weight_spec, weight_spec],
        out_specs=spec(own),
        scratch_shapes=[
            VMEM((size_y + 4, size_z + 4, size_x, lanes), F32),
            VMEM((size_y + 2, size_z + 2, size_x, lanes), F32),
        ],
        compiler_params=pltpu.CompilerParams(vmem_limit_bytes=16 << 20),
        cost_estimate=pl.CostEstimate(flops=40_000_000, bytes_accessed=4 << 20, transcendentals=1 << 20),
        name="conv_pair",
    )(flags, *arrays, first, second)


def split_three(value):
    high = value.astype(BF16)
    rest = value - high.astype(F32)
    middle = rest.astype(BF16)
    low = (rest - middle.astype(F32)).astype(BF16)
    return high.astype(F32), middle.astype(F32), low.astype(F32)


def pack_columns(maximum, denominator):
    place = lax.broadcasted_iota(jnp.int32, (maximum.shape[0], LANES), 1)
    block = jnp.zeros((maximum.shape[0], LANES), F32)
    for lane, term in enumerate(split_three(maximum) + split_three(denominator)):
        block = jnp.where(place == lane, term, block)
    return block.astype(BF16)


def unpack_columns(block):
    place = lax.broadcasted_iota(jnp.int32, block.shape, 1)
    wide = block.astype(F32)

    def term(lane):
        return jnp.sum(jnp.where(place == lane, wide, 0.0), axis=1, keepdims=True)

    return term(0) + (term(1) + term(2)), term(3) + (term(4) + term(5))


def combine(blocks):
    width = blocks[0].shape[1] - LANES
    notes = [unpack_columns(b[:, width:]) for b in blocks]
    maximum = functools.reduce(jnp.maximum, [m for m, _ in notes])
    numerator, denominator = 0.0, 0.0
    for block, (own_max, own_denominator) in zip(blocks, notes):
        factor = jnp.exp(own_max - maximum)
        numerator = numerator + factor * block[:, :width].astype(F32)
        denominator = denominator + factor * own_denominator
    return numerator, maximum, denominator


def combine_kernel(*refs):
    out = refs[-1]
    numerator, maximum, denominator = combine([r[...] for r in refs[:-1]])
    width = numerator.shape[1]
    out[:, :width] = numerator.astype(BF16)
    out[:, width:] = pack_columns(maximum, denominator)


def mean_kernel(*refs):
    out = refs[-1]
    numerator, _, denominator = combine([r[...] for r in refs[:-1]])
    out[...] = (numerator / denominator).astype(BF16)


def small_call(kernel, arrays, shape, name, flops=0):
    count = sum(a.size for a in arrays)
    return pl.pallas_call(
        kernel,
        out_shape=jax.ShapeDtypeStruct(shape, BF16),
        in_specs=[pl.BlockSpec(memory_space=VMEM)] * len(arrays),
        out_specs=pl.BlockSpec(memory_space=VMEM),
        compiler_params=pltpu.CompilerParams(vmem_limit_bytes=24 << 20),
        cost_estimate=pl.CostEstimate(flops=flops + 4 * count, bytes_accessed=2 * count, transcendentals=0),
        name=name,
    )(*arrays)


def encode_kernel(score_scale, query, own, other, out):
    width = own.shape[1]
    queries = query[...]
    pieces = [own[...], other[...]]
    scores = [dot(queries, p, ((1,), (1,))) * score_scale for p in pieces]
    maximum = jnp.maximum(
        jnp.max(scores[0], axis=1, keepdims=True), jnp.max(scores[1], axis=1, keepdims=True)
    )
    exponents = [jnp.exp(s - maximum) for s in scores]
    denominator = sum(jnp.sum(e, axis=1, keepdims=True) for e in exponents)
    numerator = sum(dot(e.astype(BF16), p, ((1,), (0,))) for e, p in zip(exponents, pieces))
    out[:, :width] = numerator.astype(BF16)
    out[:, width:] = pack_columns(maximum, denominator)


def decode_kernel(score_scale, hidden, own, other, out):
    rows = hidden[...]
    pieces = [own[...], other[...]]
    back = [dot(rows, p, ((1,), (1,))) * score_scale for p in pieces]
    maximum = jnp.maximum(
        jnp.max(back[0], axis=1, keepdims=True), jnp.max(back[1], axis=1, keepdims=True)
    )
    exponents = [jnp.exp(b - maximum) for b in back]
    denominator = sum(jnp.sum(e, axis=1, keepdims=True) for e in exponents)
    result = rows.astype(F32)
    for exponent, piece in zip(exponents, pieces):
        result = result + dot((exponent / denominator).astype(BF16), piece, ((1,), (0,)))
    out[...] = result.astype(BF16)


def local(tokens, conv_first, conv_second, kv_weight, queries):
    size_x, size_y, size_z, width = tokens.shape
    slabs, lats = lax.axis_size("slab"), lax.axis_size("lat")
    slab, lat = lax.axis_index("slab"), lax.axis_index("lat")
    score_scale = 1.0 / width**0.5
    columns = kv_weight.shape[2]
    latents = queries.shape[0]
    block = latents // (slabs * lats)
    lat_stages = radices(lats)
    upper = [(2 * stride, radix) for stride, radix in radices(slabs // 2)]

    field = jnp.transpose(tokens, (1, 2, 0, 3))

    chunk = lats * block
    own_queries = lax.dynamic_slice(queries, (slab * chunk, lat * columns), (chunk, columns))
    partial = dot(own_queries, kv_weight[0], ((1,), (1,)))

    far = pair_exchange(field, "slab", False)
    near = pair_exchange(field, "slab", True)
    for stride, radix in lat_stages:
        sent = partial.astype(BF16)
        partial = partial + sum(
            swap(sent, "lat", k * stride).astype(F32) for k in range(1, radix)
        )
    even = lat % 2 == 0
    low = jnp.stack([field[:2], near[:2], far[:2]])
    high = jnp.stack([field[-2:], near[-2:], far[-2:]])
    near_rows = pair_exchange(jnp.where(even, high, low), "lat", True)
    far_rows = pair_exchange(jnp.where(even, low, high), "lat", False)
    key_queries = gather_relative(partial.astype(BF16), "slab", upper)
    key_queries = key_queries.reshape(latents // 2, width)

    parity = slab % 2
    edges = jnp.stack([lat > 0, lat < lats - 1, slab > 0, slab < slabs - 1]).astype(jnp.int32)
    places = jnp.stack(
        [
            jnp.where(parity == 0, size_z + 2, 0),
            jnp.where(parity == 0, 0, size_z + 2),
            jnp.where(even, size_y + 2, 0),
            jnp.where(even, 0, size_y + 2),
        ]
    ).astype(jnp.int32)
    flags = jnp.concatenate([edges, places])
    hidden = hidden_of(flags, field, [near, far, near_rows, far_rows], conv_first, conv_second)
    hidden = hidden.reshape(-1, width)
    other_hidden = swap(hidden, "slab", 1)

    half = width // 2
    value_half = lax.dynamic_slice_in_dim(kv_weight[1], parity * half, half, 0)
    value_mine = gather_relative(value_half, "lat", lat_stages).reshape(lats, half, columns)
    value_other = swap(value_mine, "slab", 1)

    payload = small_call(
        functools.partial(encode_kernel, score_scale),
        [key_queries, hidden, other_hidden],
        (latents // 2, width + LANES),
        "encode",
        4 * latents * hidden.shape[0] * width,
    )
    for stride, radix in reversed(upper):
        payload = payload.reshape(radix, -1, payload.shape[-1])
        blocks = [payload[0]] + [swap(payload[k], "slab", k * stride) for k in range(1, radix)]
        payload = small_call(combine_kernel, blocks, blocks[0].shape, "combine")
    for step, (stride, radix) in enumerate(lat_stages):
        blocks = [payload] + [swap(payload, "lat", k * stride) for k in range(1, radix)]
        if step < len(lat_stages) - 1:
            payload = small_call(combine_kernel, blocks, payload.shape, "combine")
        else:
            payload = small_call(mean_kernel, blocks, (chunk, width), "mean")
    mean_mine = lax.dynamic_slice_in_dim(payload, parity * half, half, 1)
    mean_other = lax.dynamic_slice_in_dim(payload, (1 - parity) * half, half, 1)
    projected = jnp.einsum("rd,jdw->rjw", mean_mine, value_mine, preferred_element_type=F32)
    projected = projected + jnp.einsum(
        "rd,jdw->rjw", mean_other, value_other, preferred_element_type=F32
    )
    bit = 1
    while bit < lats:
        paired = projected.reshape(chunk, lats // (2 * bit), 2, bit, columns)
        projected = jnp.where((lat & bit) > 0, paired[:, :, ::-1], paired).reshape(
            chunk, lats, columns
        )
        bit *= 2
    share = projected.astype(BF16).reshape(chunk, width)
    share = gather_relative(share, "slab", upper).reshape(latents // 2, width)
    other_share = swap(share, "slab", 1)

    result = small_call(
        functools.partial(decode_kernel, score_scale),
        [hidden, share, other_share],
        hidden.shape,
        "decode",
        4 * latents * hidden.shape[0] * width,
    )
    return jnp.transpose(result.reshape(field.shape), (2, 0, 1, 3))


def solution(mesh):
    placed = (P(None, "lat", "slab", None), P(), P(), P(None, None, "lat"), P())
    return jax.shard_map(
        local, mesh=mesh, in_specs=placed, out_specs=P(None, "lat", "slab", None), check_vma=False
    )
```
